32 devices in a mesh: dp: 8 (over y, x, core), mp: 4 (over z).
Axes of the slice: x: 2, y: 2, z: 4, core: 2. Of those that a mesh axis runs over, the one named last changes fastest.
Arguments:
- inputs: float32 [16384, 1152], P('dp'), may hold values from -6 to 6
- cotangent: float32 [16384, 1152], P('dp'), may hold values from -6 to 6
- lengths: int32 [32, 3], P('dp'), may hold values from 0 to 512, as said below
- padding: int32 [32], P('dp'), may hold values from 0 to 127
- timesteps: int32 [32, 3], P('dp'), may hold values from 0 to 999
- classes: int32 [32, 3], P('dp'), may hold values from 0 to 999
- crop_head_mask: int32 [32, 3, 16], P('dp', None, 'mp'), may hold values 0 or 1
- channel_group_mask: int32 [32, 3, 16], P('dp', None, 'mp'), may hold values 0 or 1
- token_skip_flag: int32 [16384], P('dp'), may hold values 0 or 1
- time_weight: bfloat16 [256, 1152], P(None, 'mp'), may hold values from -0.375 to 0.375
- class_table: bfloat16 [1000, 1152], P(None, 'mp'), may hold values from -6 to 6
- ada_weight: bfloat16 [1152, 6, 1152], P('mp'), may hold values from -0.1875 to 0.1875
- ada_bias: float32 [6, 1152], replicated, may hold values from -4 to 4
- qkv_weight: bfloat16 [3, 1152, 1152], P(None, None, 'mp'), may hold values from -0.1875 to 0.1875
- qv_bias: float32 [2, 1152], P(None, 'mp'), may hold values from -4 to 4
- proj_weight: bfloat16 [1152, 1152], P('mp'), may hold values from -1.5 to 1.5
- proj_bias: float32 [1152], replicated, may hold values from -4 to 4
- fc1_weight: bfloat16 [1152, 4608], P(None, 'mp'), may hold values from -0.1875 to 0.1875
- fc1_bias: float32 [4608], P('mp'), may hold values from -4 to 4
- fc2_weight: bfloat16 [4608, 1152], P('mp'), may hold values from -0.09375 to 0.09375
- fc2_bias: float32 [1152], replicated, may hold values from -4 to 4
Outputs:
- layer_out: float32 [16384, 1152], P('dp')
- branch_rms: float32 [2, 16384], P(None, 'dp')
- block_input_gradient: float32 [16384, 1152], P('dp')
- time_weight_grad: float32 [256, 1152], P(None, 'mp')
- class_table_grad: float32 [1000, 1152], P(None, 'mp')
- ada_weight_grad: float32 [1152, 6, 1152], P('mp')
- ada_bias_grad: float32 [6, 1152], replicated
- qkv_weight_grad: float32 [3, 1152, 1152], P(None, None, 'mp')
- qv_bias_grad: float32 [2, 1152], P(None, 'mp')
- proj_weight_grad: float32 [1152, 1152], P('mp')
- proj_bias_grad: float32 [1152], replicated
- fc1_weight_grad: float32 [1152, 4608], P(None, 'mp')
- fc1_bias_grad: float32 [4608], P('mp')
- fc2_weight_grad: float32 [4608, 1152], P('mp')
- fc2_bias_grad: float32 [1152], replicated
The draws below stay inside these ranges and needn't reach their ends.
Inputs may be any that keep to these rules, and one draw needn't show every extreme that they name: Each row holds 1 to 3 crops in its first slots, each of 128 to 512 tokens; unused slots hold 0; a row's lengths and its padding add up to 512.
All inputs are finite; a program needn't handle non-finite values. No bound on the sum of `crop_head_mask` or of `channel_group_mask` or of `token_skip_flag` on one device may be relied on, other than what follows from the above.
Results may differ from the reference program's by a relative error of at most 0.018.
The reference program's roundings to bfloat16 on the way count: a program that leaves them out, or rounds other values in their place, can miss the bound.
Values sent between devices are 32-bit elements; how exact they have to be, the bound alone decides.
No kernel may reach another device: no remote copies, remote signals or barrier semaphores. Data moves between devices by JAX's collectives and lax.ppermute only.
A program may use at most 320 MiB of HBM per device.

```python
import math
import jax
import jax.numpy as jnp
from jax import lax

HEADS = 16
HEAD_DIM = 72
GROUP_HIDDEN = 288
TFREQ = 256
NCLASS = 1000
NSTEPS = 1000
CROPS = 3
CROP_TOKENS_LEAST = 128
MODEL_WIDTH = 1152
FF = 4608
ROW_LENGTH = 512
PACKED_ROWS = 32
TOKENS = 16384


def crop_plan(key):
    base = jax.random.fold_in(key, 23)
    key_pad, key_count, key_one, key_two = jax.random.split(base, 4)
    padding = jax.random.randint(key_pad, (PACKED_ROWS,), 0, CROP_TOKENS_LEAST)
    padding = padding.at[0].set(0).at[PACKED_ROWS - 1].set(CROP_TOKENS_LEAST - 1)
    token_count = jax.random.randint(key_count, (PACKED_ROWS,), 1, CROPS + 1).at[0].set(1)
    spare_tokens = ROW_LENGTH - padding - token_count * CROP_TOKENS_LEAST
    cut_one = jax.random.randint(key_one, (PACKED_ROWS,), 0, spare_tokens + 1)
    cut_two = jax.random.randint(key_two, (PACKED_ROWS,), 0, spare_tokens + 1)
    lower = jnp.minimum(cut_one, cut_two)
    upper = jnp.maximum(cut_one, cut_two)
    first_branch = jnp.where(token_count == 1, spare_tokens, jnp.where(token_count == 2, cut_one, lower))
    second_branch = jnp.where(token_count == 2, spare_tokens - cut_one, upper - lower)
    third = spare_tokens - upper
    extra = jnp.stack([first_branch, second_branch, third], axis=1)
    slot = jnp.arange(CROPS)[None, :]
    lengths = jnp.where(slot < token_count[:, None], CROP_TOKENS_LEAST + extra, 0)
    return (lengths.astype(jnp.int32), padding.astype(jnp.int32))


def draw_lengths(key, part):
    return crop_plan(key)[0]


def draw_padding(key, part):
    return crop_plan(key)[1]


def with_ends(values, own_key, least, top_value):
    index_at = [jax.random.randint(jax.random.fold_in(own_key, axis), (), 0, length) for axis, length in enumerate(values.shape)]
    longest = values.shape.index(max(values.shape))
    beside = index_at[:longest] + [(index_at[longest] + 1) % values.shape[longest]] + index_at[longest + 1:]
    return values.at[tuple(index_at)].set(least).at[tuple(beside)].set(top_value)


def level_of(rng, dims, cuts, least, top_value):
    gain, own = 1.0, jax.random.fold_in(rng, 6)
    for dim, parts in cuts:
        draws = jnp.exp(jax.random.uniform(jax.random.fold_in(own, dim), (parts,), jnp.float32, least / len(cuts), top_value / len(cuts)))
        gain = gain * jnp.repeat(draws, dims[dim] // parts).reshape([-1 if axis == dim else 1 for axis in range(len(dims))])
    return gain


def normal_values(stream_key, dims, scale, reach, cuts=(), kind=jnp.bfloat16):
    values = scale * jax.random.normal(stream_key, dims, jnp.float32)
    if cuts:
        values = values * level_of(stream_key, dims, cuts, -0.22, 0.18)
    return jnp.clip(values, -reach, reach).astype(kind)


def setup_inputs(seed: int = 0) -> dict:
    key_list = jax.random.split(jax.random.key(seed), 22)
    return {
        "inputs": normal_values(key_list[0], (TOKENS, MODEL_WIDTH), 1.0, 6.0, ((0, 8),), jnp.float32),
        "cotangent": normal_values(key_list[1], (TOKENS, MODEL_WIDTH), 1.0, 6.0, ((0, 8),), jnp.float32),
        "lengths": draw_lengths(jax.random.fold_in(key_list[21], 71), 0),
        "padding": draw_padding(jax.random.fold_in(key_list[21], 71), 0),
        "timesteps": with_ends(jax.random.randint(key_list[4], (PACKED_ROWS, CROPS), 0, NSTEPS), jax.random.fold_in(key_list[4], 1), 0, NSTEPS - 1).astype(jnp.int32),
        "classes": with_ends(jax.random.randint(key_list[5], (PACKED_ROWS, CROPS), 0, NCLASS), jax.random.fold_in(key_list[5], 1), 0, NCLASS - 1).astype(jnp.int32),
        "crop_head_mask": with_ends((jax.random.randint(key_list[6], (PACKED_ROWS, CROPS, HEADS), 0, 4) < 3).astype(jnp.int32), jax.random.fold_in(key_list[6], 1), 0, 1),
        "channel_group_mask": with_ends((jax.random.randint(key_list[7], (PACKED_ROWS, CROPS, HEADS), 0, 4) < 3).astype(jnp.int32), jax.random.fold_in(key_list[7], 1), 0, 1),
        "token_skip_flag": with_ends((jax.random.randint(key_list[8], (TOKENS,), 0, 4) < 1).astype(jnp.int32), jax.random.fold_in(key_list[8], 1), 0, 1),
        "time_weight": normal_values(key_list[9], (TFREQ, MODEL_WIDTH), TFREQ ** -0.5, 0.375, ((1, 4),)),
        "class_table": normal_values(key_list[10], (NCLASS, MODEL_WIDTH), 1.0, 6.0, ((1, 4),)),
        "ada_weight": normal_values(key_list[11], (MODEL_WIDTH, 6, MODEL_WIDTH), MODEL_WIDTH ** -0.5, 0.1875, ((0, 4),)),
        "ada_bias": normal_values(key_list[12], (6, MODEL_WIDTH), 0.3, 4.0, (), jnp.float32),
        "qkv_weight": normal_values(key_list[13], (3, MODEL_WIDTH, MODEL_WIDTH), MODEL_WIDTH ** -0.5, 0.1875, ((2, 4),)),
        "qv_bias": normal_values(key_list[14], (2, MODEL_WIDTH), 0.3, 4.0, ((1, 4),), jnp.float32),
        "proj_weight": normal_values(key_list[15], (MODEL_WIDTH, MODEL_WIDTH), (MODEL_WIDTH // 64) ** -0.5, 1.5, ((0, 4),)),
        "proj_bias": normal_values(key_list[16], (MODEL_WIDTH,), 0.3, 4.0, (), jnp.float32),
        "fc1_weight": normal_values(key_list[17], (MODEL_WIDTH, FF), MODEL_WIDTH ** -0.5, 0.1875, ((1, 4),)),
        "fc1_bias": normal_values(key_list[18], (FF,), 0.3, 4.0, ((0, 4),), jnp.float32),
        "fc2_weight": normal_values(key_list[19], (FF, MODEL_WIDTH), FF ** -0.5, 0.09375, ((0, 4),)),
        "fc2_bias": normal_values(key_list[20], (MODEL_WIDTH,), 0.3, 4.0, (), jnp.float32),
    }


@jax.custom_vjp
def low(v):
    return lax.optimization_barrier(v.astype(jnp.bfloat16)).astype(jnp.float32)

@jax.custom_vjp
def low_back(v):
    return v

def low_keep(v):
    return (low(v), None)

def low_pass(kept, grad):
    return (grad,)

def back_keep(v):
    return (v, None)

def back_low(kept, grad):
    return (low(grad),)
low.defvjp(low_keep, low_pass)
low_back.defvjp(back_keep, back_low)
highest = lax.Precision.HIGHEST
epsilon = 1e-06

def matmul(left, right):
    return jnp.matmul(left, right, precision=highest)

def segments(lengths, padding):
    ends = jnp.cumsum(lengths, axis=1)
    place_tokens = jnp.arange(ROW_LENGTH, dtype=jnp.int32)
    token_count = lax.optimization_barrier(jnp.sum((place_tokens[None, :, None] >= ends[:, None, :]).astype(jnp.int32), axis=2))
    valid_tokens = place_tokens[None, :] < (ROW_LENGTH - padding)[:, None]
    return jnp.where(valid_tokens, token_count, CROPS).astype(jnp.int32)

def sinusoid(steps):
    half = TFREQ // 2
    rates = jnp.exp(-math.log(10000.0) * jnp.arange(half, dtype=jnp.float32) / half)
    angles = steps.astype(jnp.float32)[:, None] * rates[None, :]
    return jnp.concatenate([jnp.cos(angles), jnp.sin(angles)], axis=1)

def layer_normalize(value_rows):
    center = value_rows - lax.optimization_barrier(jnp.mean(value_rows, axis=-1, keepdims=True))
    spread_sq = lax.optimization_barrier(jnp.mean(center * center, axis=-1, keepdims=True))
    return center * lax.rsqrt(spread_sq + epsilon)

def gelu_tanh(value_rows):
    return 0.5 * value_rows * (1.0 + jnp.tanh(0.7978845608028654 * (value_rows + 0.044715 * value_rows * value_rows * value_rows)))

def silu(value_rows):
    return value_rows / (1.0 + jnp.exp(-value_rows))

def variance(onehot, table):
    return jnp.einsum('rtc,rcf->rtf', onehot, table, precision=highest)

def attend_row(pieces):
    query, keys, values, crop_segment, mask = pieces
    length = query.shape[0]
    query_h = query.reshape(length, HEADS, HEAD_DIM)
    keys_h = keys.reshape(length, HEADS, HEAD_DIM)
    values_h = values.reshape(length, HEADS, HEAD_DIM)
    scores = jnp.einsum('qhd,khd->hqk', query_h, keys_h, precision=highest) * (1.0 / math.sqrt(HEAD_DIM))
    scores = low_back(scores)
    same = crop_segment[:, None] == crop_segment[None, :]
    scores = jnp.where(same[None], scores, -1e+30)
    peak = lax.optimization_barrier(jnp.max(scores, axis=-1, keepdims=True))
    exponent = jnp.exp(scores - peak)
    probs = exponent / lax.optimization_barrier(jnp.sum(exponent, axis=-1, keepdims=True))
    mixed = jnp.einsum('hqk,khd->qhd', low(probs), values_h, precision=highest)
    return (mixed * mask[:, :, None]).reshape(length, MODEL_WIDTH)

def forward(params, inputs, onehot, crop_segment, frequency, class_hot, head_token_mask, group_tok, keep_flags):
    time_w, table, ada_w, ada_b, qkv_w, qv_b, proj_w, proj_b, fc1_w, fc1_b, fc2_w, fc2_b = params
    condition = matmul(frequency, time_w) + matmul(class_hot, table)
    activated = low(silu(condition))
    modulate = matmul(activated, ada_w.reshape(MODEL_WIDTH, 6 * MODEL_WIDTH)).reshape(-1, 6, MODEL_WIDTH) + ada_b
    modulate = modulate.reshape(PACKED_ROWS, CROPS, 6, MODEL_WIDTH)
    first_shift, first_scale, gate_one, second_shift, second_scale, gate_two = [variance(onehot, modulate[:, :, j]) for j in range(6)]
    first_branch = low(layer_normalize(inputs) * (1.0 + first_scale) + first_shift)
    query = low_back(low(matmul(first_branch, qkv_w[0]) + qv_b[0]))
    keys = low_back(low(matmul(first_branch, qkv_w[1])))
    values = low_back(low(matmul(first_branch, qkv_w[2]) + qv_b[1]))
    mixed = lax.map(jax.checkpoint(attend_row), (query, keys, values, crop_segment, head_token_mask))
    merged = low_back(low(mixed))
    branch_attn = low_back(matmul(merged, proj_w) + proj_b)
    middle_state = inputs + gate_one * branch_attn
    second_branch = low(layer_normalize(middle_state) * (1.0 + second_scale) + second_shift)
    hidden = low_back(matmul(second_branch, fc1_w) + fc1_b)
    gated = low(gelu_tanh(hidden) * group_tok)
    branch_mlp = low_back(matmul(gated, fc2_w) + fc2_b)
    result = middle_state + gate_two * keep_flags * branch_mlp
    rms = jnp.stack([jnp.sqrt(lax.optimization_barrier(jnp.mean(branch_attn * branch_attn, axis=-1)) + epsilon), jnp.sqrt(lax.optimization_barrier(jnp.mean(branch_mlp * branch_mlp, axis=-1)) + epsilon)])
    return (result, rms)

def reference(inputs, cotangent, lengths, padding, timesteps, classes, crop_head_mask, channel_group_mask, token_skip_flag, time_weight, class_table, ada_weight, ada_bias, qkv_weight, qv_bias, proj_weight, proj_bias, fc1_weight, fc1_bias, fc2_weight, fc2_bias):
    crop_segment = segments(lengths, padding)
    onehot = (crop_segment[:, :, None] == jnp.arange(CROPS, dtype=jnp.int32)[None, None, :]).astype(jnp.float32)
    frequency = low(sinusoid(timesteps.reshape(-1)))
    class_hot = (classes.reshape(-1)[:, None] == jnp.arange(NCLASS, dtype=jnp.int32)[None, :]).astype(jnp.float32)
    head_token_mask = variance(onehot, crop_head_mask.astype(jnp.float32))
    group_tok = jnp.repeat(variance(onehot, channel_group_mask.astype(jnp.float32)), GROUP_HIDDEN, axis=2)
    keep_flags = (1 - token_skip_flag).astype(jnp.float32).reshape(PACKED_ROWS, ROW_LENGTH, 1)
    params = tuple((w.astype(jnp.float32) for w in (time_weight, class_table, ada_weight, ada_bias, qkv_weight, qv_bias, proj_weight, proj_bias, fc1_weight, fc1_bias, fc2_weight, fc2_bias)))
    input_rows = inputs.reshape(PACKED_ROWS, ROW_LENGTH, MODEL_WIDTH)

    def wrapped(weights, values):
        return forward(weights, values, onehot, crop_segment, frequency, class_hot, head_token_mask, group_tok, keep_flags)
    result, pull_gradient, rms = jax.vjp(wrapped, params, input_rows, has_aux=True)
    gradient_list, block_input_gradient = pull_gradient(cotangent.reshape(PACKED_ROWS, ROW_LENGTH, MODEL_WIDTH))
    return (result.reshape(TOKENS, MODEL_WIDTH), rms.reshape(2, TOKENS), block_input_gradient.reshape(TOKENS, MODEL_WIDTH), gradient_list[0], gradient_list[1], gradient_list[2], gradient_list[3], gradient_list[4], gradient_list[5], gradient_list[6], gradient_list[7], gradient_list[8], gradient_list[9], gradient_list[10], gradient_list[11])
```

```python
import functools
import math

import jax
import jax.numpy as jnp
from jax import lax
from jax.experimental import pallas as pl
from jax.experimental.pallas import tpu as pltpu
from jax.sharding import PartitionSpec as P

HEAD_DIM = 72
GROUP_HIDDEN = 288
TFREQ = 256
NCLASS = 1000
CROPS = 3
ROW_LENGTH = 512
MIB = 1 << 20

highest = lax.Precision.HIGHEST
epsilon = 1e-06
f32 = jnp.float32
bf16 = jnp.bfloat16
SCALE = 1.0 / math.sqrt(HEAD_DIM)
LOG2E = math.log2(math.e)


def segments(lengths, padding):
    ends = jnp.cumsum(lengths, axis=1)
    place_tokens = jnp.arange(ROW_LENGTH, dtype=jnp.int32)
    token_count = jnp.sum(
        (place_tokens[None, :, None] >= ends[:, None, :]).astype(jnp.int32), axis=2
    )
    valid_tokens = place_tokens[None, :] < (ROW_LENGTH - padding)[:, None]
    return jnp.where(valid_tokens, token_count, CROPS)


def sinusoid(steps):
    half = TFREQ // 2
    rates = jnp.exp(-math.log(10000.0) * jnp.arange(half, dtype=f32) / half)
    angles = steps.astype(f32)[:, None] * rates[None, :]
    return jnp.concatenate([jnp.cos(angles), jnp.sin(angles)], axis=1)


def silu(value_rows):
    return value_rows / (1.0 + jnp.exp(-value_rows))


def product(left, right):
    return jnp.dot(left, right, preferred_element_type=f32)


def exact(left, right):
    return jnp.dot(left, right, precision=highest)


def dot_as(left, right, left_dim, right_dim):
    return lax.dot_general(
        left, right, (((left_dim,), (right_dim,)), ((), ())), preferred_element_type=f32
    )


def tree_sum(values):
    values = list(values)
    while len(values) > 1:
        values = [
            values[i] + values[i + 1] if i + 1 < len(values) else values[i]
            for i in range(0, len(values), 2)
        ]
    return values[0]


def pick(table_ref, j, seg):
    result = jnp.where(seg == 2, table_ref[0, j, 2:3, :], 0.0)
    result = jnp.where(seg == 1, table_ref[0, j, 1:2, :], result)
    return jnp.where(seg == 0, table_ref[0, j, 0:1, :], result)


def normal(rows):
    center = rows - jnp.mean(rows, axis=-1, keepdims=True)
    inverse = lax.rsqrt(jnp.mean(center * center, axis=-1, keepdims=True) + epsilon)
    return center * inverse, inverse


def normal_back(grad, xhat, inverse):
    return (
        grad
        - jnp.mean(grad, axis=-1, keepdims=True)
        - xhat * jnp.mean(grad * xhat, axis=-1, keepdims=True)
    ) * inverse


def crop_sums(values, seg):
    return [
        jnp.sum(jnp.where(seg == slot, values, 0.0), axis=0, keepdims=True) for slot in range(CROPS)
    ]


def first_kernel(x_ref, seg_ref, mod_ref, out_ref):
    xhat, _ = normal(x_ref[...])
    seg = seg_ref[...]
    out_ref[...] = (xhat * (1.0 + pick(mod_ref, 1, seg)) + pick(mod_ref, 0, seg)).astype(bf16)


def attend_kernel(n_pieces, heads, *refs):
    if n_pieces:
        place_ref, refs = refs[0], refs[1:]
    first_ref, segk_ref, segq_ref, mask_ref, bias_ref = refs[:5]
    weight_refs, refs = refs[5 : 5 + max(n_pieces, 1)], refs[5 + max(n_pieces, 1) :]
    if n_pieces:
        qkv_ref, mixed_ref, lse_ref, weight_ref, neg_ref, acc_ref = refs

        @pl.when(pl.program_id(0) == 0)
        def _():
            rows = weight_refs[0].shape[0]
            for m in range(n_pieces):
                at = pl.multiple_of((place_ref[0] ^ m) * rows, 16)
                weight_ref[pl.ds(at, rows), :] = weight_refs[m][...].astype(bf16)
    else:
        qkv_ref, mixed_ref, lse_ref, neg_ref, acc_ref = refs
        weight_ref = weight_refs[0]
    width = heads * HEAD_DIM
    first = first_ref[...]
    for part in range(3):
        rows = pl.ds(part * width, width)
        out = dot_as(weight_ref[rows, :], first, 1, 1) + bias_ref[rows, :]
        for h in range(heads):
            qkv_ref[part * heads + h] = out[h * HEAD_DIM : (h + 1) * HEAD_DIM].astype(bf16)
    neg_ref[...] = jnp.where(segk_ref[...] == segq_ref[0], 0.0, -1e30)
    for h in range(heads):
        query, keys, values = qkv_ref[h], qkv_ref[heads + h], qkv_ref[2 * heads + h]
        scores = dot_as(keys, query, 0, 0) * (SCALE * LOG2E) + neg_ref[...]
        peak = jnp.max(scores, axis=0, keepdims=True)
        exponent = jnp.exp2(scores - peak)
        total = jnp.sum(exponent, axis=0, keepdims=True)
        probs = (exponent * (1.0 / total)).astype(bf16)
        acc_ref[pl.ds(h * HEAD_DIM, HEAD_DIM), :] = (
            dot_as(values, probs, 1, 0) * mask_ref[0, h : h + 1, :]
        )
        lse_ref[0, h : h + 1, :] = peak + jnp.log2(total)
    mixed_ref[...] = acc_ref[...].astype(bf16)


def middle_kernel(parts, hw, *refs):
    mixed_refs, refs = refs[:parts], refs[parts:]
    weight_refs, refs = refs[:parts], refs[parts:]
    (
        bias_ref,
        x_ref,
        cot_ref,
        seg_ref,
        keep_ref,
        mod_ref,
        branch_ref,
        middle_ref,
        second_ref,
        mgrad_ref,
        rms_ref,
        gsum_ref,
    ) = refs
    branch = (
        tree_sum(
            dot_as(mixed_refs[k][...], weight_refs[k][pl.ds(3 * hw, hw), :], 0, 0)
            for k in range(parts)
        )
        + bias_ref[...]
    )
    seg = seg_ref[...]
    branch_ref[...] = branch
    rms_ref[...] = jnp.sqrt(jnp.mean(branch * branch, axis=-1, keepdims=True) + epsilon)
    middle = x_ref[...] + pick(mod_ref, 2, seg) * branch
    middle_ref[...] = middle
    xhat, _ = normal(middle)
    second_ref[...] = (xhat * (1.0 + pick(mod_ref, 4, seg)) + pick(mod_ref, 3, seg)).astype(bf16)
    mgrad = (pick(mod_ref, 5, seg) * keep_ref[...] * cot_ref[...]).astype(bf16)
    mgrad_ref[...] = mgrad

    @pl.when(pl.program_id(0) + pl.program_id(1) == 0)
    def _():
        gsum_ref[...] = jnp.zeros_like(gsum_ref)

    gsum_ref[...] += jnp.sum(mgrad.astype(f32), axis=0, keepdims=True)


def mlp_kernel(n_add, packed, keep_own, *refs):
    second_ref, mgrad_ref, seg_ref, gmask_ref, bias_ref = refs[:5]
    refs = refs[5:]
    if packed:
        pack_ref, refs = refs[0], refs[1:]
    else:
        w1_ref, w2_ref, refs = refs[0], refs[1], refs[2:]
    adds, refs = refs[: 2 * n_add], refs[2 * n_add :]
    bm_ref, sg_ref, refs = refs[0], refs[1], refs[2:]
    if keep_own:
        gated_ref, hgrad_ref, hsum_ref, refs = refs[0], refs[1], refs[2], refs[3:]

        @pl.when(pl.program_id(0) + pl.program_id(1) == 0)
        def _():
            hsum_ref[...] = jnp.zeros_like(hsum_ref)

    if packed:
        w1_ref, w2_ref = refs

        @pl.when(pl.program_id(0) + pl.program_id(1) == 0)
        def _():
            rows = w1_ref.shape[0] // packed
            for d in range(packed):
                w1_ref[pl.ds(d * rows, rows), :] = pack_ref[pl.ds(2 * d * rows, rows), :].astype(bf16)
                w2_ref[pl.ds(d * rows, rows), :] = pack_ref[
                    pl.ds((2 * d + 1) * rows, rows), :
                ].astype(bf16)

    second, mgrad, seg = second_ref[...], mgrad_ref[...], seg_ref[...]
    units = w1_ref.shape[0]
    bm = sg = None
    for at in range(0, units, 512):
        cols = slice(at, min(at + 512, units))
        u = dot_as(second, w1_ref[cols, :], 1, 1) + bias_ref[:, cols]
        up = dot_as(mgrad, w2_ref[cols, :], 1, 1)
        mask = jnp.where(seg == 2, gmask_ref[0, 2:3, cols], 0.0)
        mask = jnp.where(seg == 1, gmask_ref[0, 1:2, cols], mask)
        mask = jnp.where(seg == 0, gmask_ref[0, 0:1, cols], mask)
        square = u * u
        t = jnp.tanh(0.7978845608028654 * u * (1.0 + 0.044715 * square))
        half = 0.5 * (1.0 + t)
        slope = half + (0.5 * u) * (1.0 - t * t) * (
            0.7978845608028654 + (3.0 * 0.044715 * 0.7978845608028654) * square
        )
        gated = (u * half * mask).astype(bf16)
        hgrad = (up * mask * slope).astype(bf16)
        if keep_own:
            gated_ref[:, cols] = gated
            hgrad_ref[:, cols] = hgrad
            hsum_ref[:, cols] += jnp.sum(hgrad.astype(f32), axis=0, keepdims=True)
        bm_part = dot_as(gated, w2_ref[cols, :], 1, 0)
        sg_part = dot_as(hgrad, w1_ref[cols, :], 1, 0)
        bm = bm_part if bm is None else bm + bm_part
        sg = sg_part if sg is None else sg + sg_part
    for i in range(n_add):
        bm = bm + adds[2 * i][...]
        sg = sg + adds[2 * i + 1][...]
    bm_ref[...] = bm
    sg_ref[...] = sg


def turn_kernel(
    middle_ref,
    branch_ref,
    bm_ref,
    sg_ref,
    cot_ref,
    seg_ref,
    keep_ref,
    mod_ref,
    bias_ref,
    out_ref,
    mg_ref,
    ag_ref,
    rms_ref,
    sums_ref,
    asum_ref,
):
    seg, keep, cot = seg_ref[...], keep_ref[...], cot_ref[...]
    bm = bm_ref[...] + bias_ref[...]
    rms_ref[...] = jnp.sqrt(jnp.mean(bm * bm, axis=-1, keepdims=True) + epsilon)
    middle = middle_ref[...]
    kept = keep * bm
    out_ref[...] = middle + pick(mod_ref, 5, seg) * kept
    xhat, inverse = normal(middle)
    sg = sg_ref[...]
    mg = cot + normal_back(sg * (1.0 + pick(mod_ref, 4, seg)), xhat, inverse)
    mg_ref[...] = mg
    ag = (pick(mod_ref, 2, seg) * mg).astype(bf16)
    ag_ref[...] = ag

    @pl.when(pl.program_id(1) == 0)
    def _():
        sums_ref[...] = jnp.zeros_like(sums_ref)

    @pl.when(pl.program_id(0) + pl.program_id(1) == 0)
    def _():
        asum_ref[...] = jnp.zeros_like(asum_ref)

    asum_ref[...] += jnp.sum(ag.astype(f32), axis=0, keepdims=True)
    for j, values in enumerate((mg * branch_ref[...], sg, sg * xhat, cot * kept)):
        for slot, row in enumerate(crop_sums(values, seg)):
            sums_ref[0, j, slot : slot + 1, :] += row


def attend_back_kernel(parts, heads, *refs):
    ag_ref, first_ref, mixed_ref, segk_ref, segq_ref = refs[:5]
    refs = refs[5:]
    mask_refs, refs = refs[:parts], refs[parts:]
    lse_refs, refs = refs[:parts], refs[parts:]
    qkv_refs, refs = refs[:parts], refs[parts:]
    weight_refs, refs = refs[:parts], refs[parts:]
    fg_ref, wgrad_ref, bsum_ref, neg_ref, up_ref, acc_ref = refs
    width = heads * HEAD_DIM
    neg_ref[...] = jnp.where(segk_ref[...] == segq_ref[0], 0.0, -1e30)
    ag = ag_ref[...]

    @pl.when(pl.program_id(0) == 0)
    def _():
        wgrad_ref[...] = jnp.zeros_like(wgrad_ref)
        bsum_ref[...] = jnp.zeros_like(bsum_ref)

    grads = []
    for k in range(parts):
        up = dot_as(weight_refs[k][pl.ds(3 * width, width), :], ag, 1, 1)
        for h in range(heads):
            mask = mask_refs[k][0, h : h + 1, :]
            up_ref[h] = (up[h * HEAD_DIM : (h + 1) * HEAD_DIM].astype(bf16).astype(f32) * mask).astype(bf16)
        for h in range(heads):
            query, keys, values = (qkv_refs[k][i * heads + h] for i in range(3))
            upstream = up_ref[h]
            scores = dot_as(keys, query, 0, 0) * (SCALE * LOG2E) + neg_ref[...]
            probs = jnp.exp2(scores - lse_refs[k][0, h : h + 1, :])
            prob_grad = dot_as(values, upstream, 0, 0)
            center = jnp.sum(probs * prob_grad, axis=0, keepdims=True)
            score_grad = (probs * (prob_grad - center)).astype(bf16)
            at = h * HEAD_DIM
            acc_ref[pl.ds(at, HEAD_DIM), :] = dot_as(keys, score_grad, 1, 0) * SCALE
            acc_ref[pl.ds(width + at, HEAD_DIM), :] = dot_as(query, score_grad, 1, 1) * SCALE
            acc_ref[pl.ds(2 * width + at, HEAD_DIM), :] = dot_as(upstream, probs.astype(bf16), 1, 1)
        back = acc_ref[...].astype(bf16)
        grads.append(dot_as(back, weight_refs[k][pl.ds(0, 3 * width), :], 0, 0))
        if k == 0:
            wgrad_ref[pl.ds(0, 3 * width), :] += dot_as(back, first_ref[...], 1, 0)
            wgrad_ref[pl.ds(3 * width, width), :] += dot_as(mixed_ref[...], ag, 1, 0)
            bsum_ref[...] += jnp.sum(back.astype(f32), axis=1, keepdims=True)
    fg_ref[...] = tree_sum(grads)


def last_kernel(x_ref, fg_ref, mg_ref, seg_ref, mod_ref, out_ref, sums_ref):
    seg = seg_ref[...]
    xhat, inverse = normal(x_ref[...])
    fg = fg_ref[...]
    out_ref[...] = mg_ref[...] + normal_back(fg * (1.0 + pick(mod_ref, 1, seg)), xhat, inverse)

    @pl.when(pl.program_id(1) == 0)
    def _():
        sums_ref[...] = jnp.zeros_like(sums_ref)

    for j, values in enumerate((fg, fg * xhat)):
        for slot, row in enumerate(crop_sums(values, seg)):
            sums_ref[0, j, slot : slot + 1, :] += row


def call(kernel, name, grid, ins, outs, scratch=(), prefetch=(), cost=None, aliases=None, vmem=58):
    arrays = [a for a, _ in ins]
    return pl.pallas_call(
        kernel,
        name=name,
        grid_spec=pltpu.PrefetchScalarGridSpec(
            num_scalar_prefetch=len(prefetch),
            grid=grid,
            in_specs=[s for _, s in ins],
            out_specs=[s for _, s in outs],
            scratch_shapes=list(scratch),
        ),
        out_shape=[a for a, _ in outs],
        input_output_aliases=aliases or {},
        cost_estimate=cost,
        compiler_params=pltpu.CompilerParams(
            dimension_semantics=("arbitrary",) * len(grid), vmem_limit_bytes=vmem * MIB
        ),
    )(*prefetch, *arrays)


def cost_of(flops, moved, transcendentals=0):
    return pl.CostEstimate(
        flops=int(flops), bytes_accessed=int(moved), transcendentals=int(transcendentals)
    )


def whole(array):
    nd = array.ndim
    return (array, pl.BlockSpec(array.shape, lambda *_: (0,) * nd, pipeline_mode=pl.Buffered(1)))


def shape(dims, kind=f32):
    return jax.ShapeDtypeStruct(tuple(dims), kind)


def shards(
    dp_size,
    mp_size,
    inputs,
    cotangent,
    lengths,
    padding,
    timesteps,
    classes,
    crop_head_mask,
    channel_group_mask,
    token_skip_flag,
    time_weight,
    class_table,
    ada_weight,
    ada_bias,
    qkv_weight,
    qv_bias,
    proj_weight,
    proj_bias,
    fc1_weight,
    fc1_bias,
    fc2_weight,
    fc2_bias,
):
    rows = lengths.shape[0]
    tokens, width = inputs.shape
    hw = qkv_weight.shape[2]
    heads = hw // HEAD_DIM
    units = fc2_weight.shape[0]
    groups = channel_group_mask.shape[2]
    place = lax.axis_index("dp")
    mine = lax.axis_index("mp")

    def across_mp(x, k):
        return lax.ppermute(x, "mp", [(i, i ^ k) for i in range(mp_size)])

    def across_dp(x, m):
        return lax.ppermute(x, "dp", [(i, i ^ m) for i in range(dp_size)])

    attn_own = jnp.concatenate(
        [jnp.swapaxes(qkv_weight, 1, 2).reshape(3 * hw, width), proj_weight], axis=0
    )
    fc1_own = fc1_weight.T
    ring = dp_size == 8 and (4 * hw) % (16 * dp_size) == 0 and units % (16 * dp_size) == 0
    attn_parts, mlp_parts = [attn_own], [(fc1_own, fc2_weight)]
    if ring:
        a_rows, m_rows = 4 * hw // dp_size, units // dp_size
        a_slice = lax.dynamic_slice_in_dim(attn_own, place * a_rows, a_rows).astype(f32)
        m_slice = jnp.concatenate(
            [
                lax.dynamic_slice_in_dim(fc1_own, place * m_rows, m_rows),
                lax.dynamic_slice_in_dim(fc2_weight, place * m_rows, m_rows),
            ]
        ).astype(f32)
        for k in range(1, mp_size):
            piece = across_mp(a_slice, k)
            near, far = (2, 4) if k % 2 else (4, 2)
            side = across_dp(piece, near)
            plane = {0: piece, near: side, far: across_dp(piece, far), 6: across_dp(side, far)}
            for m in (0, 2, 4, 6):
                plane[m + 1] = across_dp(plane[m], 1)
            attn_parts.append([plane[m] for m in range(8)])
        for k in range(1, mp_size):
            mlp_parts.append(lax.all_gather(across_mp(m_slice, k), "dp", tiled=True))
    else:
        attn_all = lax.all_gather(attn_own.astype(f32), "mp")
        fc1_all = lax.all_gather(fc1_own.astype(f32), "mp")
        fc2_all = lax.all_gather(fc2_weight.astype(f32), "mp")

        def take(stack, k):
            block = (1,) + stack.shape[1:]
            return call(
                lambda _, x_ref, out_ref: out_ref.__setitem__(..., x_ref[0].astype(bf16)),
                "narrow",
                (1,),
                [(stack, pl.BlockSpec(block, lambda i, at: (at[0], 0, 0)))],
                [(shape(stack.shape[1:], bf16), pl.BlockSpec(stack.shape[1:], lambda i, at: (0, 0)))],
                prefetch=[(mine ^ k).reshape(1)],
            )[0]

        for k in range(1, mp_size):
            attn_parts.append(take(attn_all, k))
            mlp_parts.append((take(fc1_all, k), take(fc2_all, k)))

    seg = segments(lengths, padding)
    many = rows * CROPS
    keys_all = lax.all_gather(
        jnp.stack([timesteps.reshape(-1), classes.reshape(-1)]), "dp", axis=1, tiled=True
    )

    def conditioned(steps, labels):
        frequency = sinusoid(steps).astype(bf16)
        class_hot = (labels[:, None] == jnp.arange(NCLASS, dtype=jnp.int32)[None, :]).astype(bf16)
        condition = product(frequency, time_weight) + product(class_hot, class_table)
        return frequency, class_hot, condition

    _, _, condition = conditioned(timesteps.reshape(-1), classes.reshape(-1))
    activated = silu(condition).astype(bf16)
    flat_ada = ada_weight.reshape(hw, 6 * width)
    modulate = lax.psum(product(activated, flat_ada), "mp").reshape(many, 6, width) + ada_bias
    table = jnp.pad(
        modulate.reshape(rows, CROPS, 6, width).transpose(0, 2, 1, 3),
        ((0, 0), (0, 0), (0, 8 - CROPS), (0, 0)),
    )

    n_head, n_group = rows * CROPS * heads, rows * CROPS * groups
    aux_own = jnp.concatenate(
        [
            crop_head_mask.astype(f32).reshape(-1),
            channel_group_mask.astype(f32).reshape(-1),
            qv_bias[0],
            jnp.zeros((hw,), f32),
            qv_bias[1],
            fc1_bias,
        ]
    )
    aux = [aux_own] + [across_mp(aux_own, k) for k in range(1, mp_size)]
    seg_col = seg.reshape(tokens, 1)
    seg_row = seg.reshape(rows, 1, ROW_LENGTH)
    keep_col = (1 - token_skip_flag).astype(f32).reshape(tokens, 1)
    head_masks, group_masks, qkv_biases, fc1_biases = [], [], [], []
    for part in aux:
        head = part[:n_head].reshape(rows, CROPS, heads)
        group = part[n_head : n_head + n_group].reshape(rows, CROPS, groups)
        rest = part[n_head + n_group :]
        by_slot = [
            jnp.where(seg_row == slot, head[:, slot, :, None], 0.0) for slot in range(CROPS)
        ]
        head_masks.append(sum(by_slot))
        group_masks.append(
            jnp.pad(jnp.repeat(group, GROUP_HIDDEN, axis=2), ((0, 0), (0, 8 - CROPS), (0, 0)))
        )
        qkv_biases.append(rest[: 3 * hw].reshape(3 * hw, 1))
        fc1_biases.append(rest[3 * hw :].reshape(1, units))

    tile = 256
    per_row = ROW_LENGTH // tile

    def tok(kind, cols=width):
        return (
            shape((tokens, cols), kind),
            pl.BlockSpec((tile, cols), lambda r, i: (r * per_row + i, 0)),
        )

    def tok_in(array):
        return (
            array,
            pl.BlockSpec((tile, array.shape[1]), lambda r, i: (r * per_row + i, 0)),
        )

    def once(dims, kind=f32):
        nd = len(dims)
        return (shape(dims, kind), pl.BlockSpec(dims, lambda *_: (0,) * nd))

    table_in = (table, pl.BlockSpec((1, 6, 8, width), lambda r, i: (r, 0, 0, 0)))
    grid2 = (rows, per_row)
    grid1 = (rows,)

    def row_in(array, dims):
        nd = len(dims)
        return (array, pl.BlockSpec(dims, lambda r, *_: (r,) + (0,) * (nd - 1)))

    def lane_in(array, dims):
        nd = len(dims)
        return (array, pl.BlockSpec(dims, lambda r, *_: (0,) * (nd - 1) + (r,)))

    (first,) = call(
        first_kernel,
        "first",
        grid2,
        [tok_in(inputs), tok_in(seg_col), table_in],
        [tok(bf16)],
        cost=cost_of(20 * tokens * width, 6 * tokens * width),
    )

    pair = tokens * ROW_LENGTH * heads
    qkv_t, mixed_t, lse, attn_w = [], [], [], []
    for k in range(mp_size):
        part = attn_parts[k]
        pieces = part if isinstance(part, list) else [part]
        n_pieces = len(part) if isinstance(part, list) else 0
        outs = [
            lane_in(shape((3 * heads, HEAD_DIM, tokens), bf16), (3 * heads, HEAD_DIM, ROW_LENGTH)),
            lane_in(shape((hw, tokens), bf16), (hw, ROW_LENGTH)),
            row_in(shape((rows, heads, ROW_LENGTH)), (1, heads, ROW_LENGTH)),
        ]
        if n_pieces:
            outs.append(once((4 * hw, width), bf16))
        result = call(
            functools.partial(attend_kernel, n_pieces, heads),
            "attend",
            grid1,
            [
                row_in(first, (ROW_LENGTH, width)),
                row_in(seg_col, (ROW_LENGTH, 1)),
                row_in(seg_row, (1, 1, ROW_LENGTH)),
                row_in(head_masks[k], (1, heads, ROW_LENGTH)),
                whole(qkv_biases[k]),
            ]
            + [whole(p) for p in pieces],
            outs,
            scratch=[
                pltpu.VMEM((ROW_LENGTH, ROW_LENGTH), f32),
                pltpu.VMEM((hw, ROW_LENGTH), f32),
            ],
            prefetch=[place.reshape(1)] if n_pieces else [],
            cost=cost_of(
                2 * tokens * width * 3 * hw + 4 * pair * HEAD_DIM,
                2 * tokens * width + 8 * tokens * hw + 4 * 4 * hw * width,
                pair,
            ),
        )
        qkv_t.append(result[0])
        mixed_t.append(result[1])
        lse.append(result[2])
        attn_w.append(result[3] if n_pieces else part)

    branch, middle, second, mlp_grad, rms_one, fc2_bias_sum = call(
        functools.partial(middle_kernel, mp_size, hw),
        "middle",
        grid2,
        [
            (m, pl.BlockSpec((hw, tile), lambda r, i: (0, r * per_row + i))) for m in mixed_t
        ]
        + [whole(w) for w in attn_w]
        + [
            whole(proj_bias.reshape(1, width)),
            tok_in(inputs),
            tok_in(cotangent),
            tok_in(seg_col),
            tok_in(keep_col),
            table_in,
        ],
        [tok(f32), tok(f32), tok(bf16), tok(bf16), tok(f32, 1), once((1, width))],
        cost=cost_of(2 * tokens * width * hw * mp_size, 22 * tokens * width),
    )

    stack = []
    gated = hidden_grad = fc1_bias_sum = None
    for k in range(mp_size):
        part = mlp_parts[k]
        packed = 0 if isinstance(part, tuple) else dp_size
        merged = []
        level = 0
        while stack and stack[-1][0] == level:
            merged.append(stack.pop()[1])
            level += 1
        outs = [tok(f32), tok(f32)]
        if k == 0:
            outs += [tok(bf16, units), tok(bf16, units), once((1, units))]
        n_in = 5 + (1 if packed else 2)
        result = call(
            functools.partial(mlp_kernel, len(merged), packed, k == 0),
            "mlp",
            grid2,
            [
                tok_in(second),
                tok_in(mlp_grad),
                tok_in(seg_col),
                (group_masks[k], pl.BlockSpec((1, 8, units), lambda r, i: (r, 0, 0))),
                whole(fc1_biases[k]),
            ]
            + ([whole(part)] if packed else [whole(w) for w in part])
            + [tok_in(a) for pair_of in merged for a in pair_of],
            outs,
            scratch=[pltpu.VMEM((units, width), bf16)] * 2 if packed else [],
            aliases={n_in: 0, n_in + 1: 1} if merged else {},
            cost=cost_of(8 * tokens * width * units, 20 * tokens * width, tokens * units),
        )
        stack.append((level, (result[0], result[1])))
        if k == 0:
            gated, hidden_grad, fc1_bias_sum = result[2:]
    ((_, (branch_mlp, second_grad)),) = stack

    layer_out, middle_grad, attn_grad, rms_two, sums_mid, proj_bias_sum = call(
        turn_kernel,
        "turn",
        grid2,
        [
            tok_in(middle),
            tok_in(branch),
            tok_in(branch_mlp),
            tok_in(second_grad),
            tok_in(cotangent),
            tok_in(seg_col),
            tok_in(keep_col),
            table_in,
            whole(fc2_bias.reshape(1, width)),
        ],
        [
            tok(f32),
            tok(f32),
            tok(bf16),
            tok(f32, 1),
            (shape((rows, 4, 8, width)), pl.BlockSpec((1, 4, 8, width), lambda r, i: (r, 0, 0, 0))),
            once((1, width)),
        ],
        cost=cost_of(60 * tokens * width, 30 * tokens * width),
    )

    fc2_weight_grad = dot_as(gated, mlp_grad, 0, 0)
    fc1_weight_grad = dot_as(second, hidden_grad, 0, 0)

    first_grad, attn_w_grad, qkv_bias_sum = call(
        functools.partial(attend_back_kernel, mp_size, heads),
        "attend_back",
        grid1,
        [
            row_in(attn_grad, (ROW_LENGTH, width)),
            row_in(first, (ROW_LENGTH, width)),
            lane_in(mixed_t[0], (hw, ROW_LENGTH)),
            row_in(seg_col, (ROW_LENGTH, 1)),
            row_in(seg_row, (1, 1, ROW_LENGTH)),
        ]
        + [row_in(m, (1, heads, ROW_LENGTH)) for m in head_masks]
        + [row_in(v, (1, heads, ROW_LENGTH)) for v in lse]
        + [lane_in(q, (3 * heads, HEAD_DIM, ROW_LENGTH)) for q in qkv_t]
        + [whole(w) for w in attn_w],
        [
            row_in(shape((tokens, width)), (ROW_LENGTH, width)),
            once((4 * hw, width)),
            once((3 * hw, 1)),
        ],
        scratch=[
            pltpu.VMEM((ROW_LENGTH, ROW_LENGTH), f32),
            pltpu.VMEM((heads, HEAD_DIM, ROW_LENGTH), bf16),
            pltpu.VMEM((3 * hw, ROW_LENGTH), f32),
        ],
        cost=cost_of(
            mp_size * (8 * tokens * width * hw + 10 * pair * HEAD_DIM),
            20 * tokens * width,
            mp_size * pair,
        ),
    )

    block_input_gradient, sums_first = call(
        last_kernel,
        "last",
        grid2,
        [tok_in(inputs), tok_in(first_grad), tok_in(middle_grad), tok_in(seg_col), table_in],
        [
            tok(f32),
            (shape((rows, 2, 8, width)), pl.BlockSpec((1, 2, 8, width), lambda r, i: (r, 0, 0, 0))),
        ],
        cost=cost_of(40 * tokens * width, 16 * tokens * width),
    )

    local_grad = (
        jnp.concatenate([sums_first, sums_mid], axis=1)[:, :, :CROPS]
        .transpose(0, 2, 1, 3)
        .reshape(many, 6 * width)
    )
    flat_grad = lax.all_gather(local_grad, "dp", tiled=True)
    frequency, class_hot, condition_all = conditioned(keys_all[0], keys_all[1])
    activated_f, silu_pull = jax.vjp(silu, condition_all)
    activated_all = activated_f.astype(bf16)
    ada_bias_grad = jnp.sum(flat_grad, axis=0).reshape(6, width)
    ada_weight_grad = exact(activated_all.astype(f32).T, flat_grad).reshape(hw, 6, width)
    activated_grad = exact(flat_grad, flat_ada.astype(f32).T)
    (condition_grad,) = silu_pull(activated_grad)
    time_weight_grad = exact(frequency.astype(f32).T, condition_grad)
    class_table_grad = exact(class_hot.astype(f32).T, condition_grad)

    fc2_weight_grad, fc1_weight_grad = lax.psum((fc2_weight_grad, fc1_weight_grad), "dp")
    attn_w_grad, qkv_bias_sum, proj_bias_sum, fc1_bias_sum, fc2_bias_sum = lax.psum(
        (
            attn_w_grad,
            qkv_bias_sum.reshape(3, hw),
            proj_bias_sum.reshape(width),
            fc1_bias_sum.reshape(units),
            fc2_bias_sum.reshape(width),
        ),
        "dp",
    )
    qkv_weight_grad = jnp.swapaxes(attn_w_grad[: 3 * hw].reshape(3, hw, width), 1, 2)
    return (
        layer_out,
        jnp.concatenate([rms_one, rms_two], axis=1).T,
        block_input_gradient,
        time_weight_grad,
        class_table_grad,
        ada_weight_grad,
        ada_bias_grad,
        qkv_weight_grad,
        jnp.stack([qkv_bias_sum[0], qkv_bias_sum[2]]),
        attn_w_grad[3 * hw :],
        proj_bias_sum,
        fc1_weight_grad,
        fc1_bias_sum,
        fc2_weight_grad,
        fc2_bias_sum,
    )


def solution(mesh):
    in_specs = (
        P("dp", None),
        P("dp", None),
        P("dp", None),
        P("dp"),
        P("dp", None),
        P("dp", None),
        P("dp", None, "mp"),
        P("dp", None, "mp"),
        P("dp"),
        P(None, "mp"),
        P(None, "mp"),
        P("mp", None, None),
        P(),
        P(None, None, "mp"),
        P(None, "mp"),
        P("mp", None),
        P(),
        P(None, "mp"),
        P("mp"),
        P("mp", None),
        P(),
    )
    out_specs = (
        P("dp", None),
        P(None, "dp"),
        P("dp", None),
        P(None, "mp"),
        P(None, "mp"),
        P("mp", None, None),
        P(),
        P(None, None, "mp"),
        P(None, "mp"),
        P("mp", None),
        P(),
        P(None, "mp"),
        P("mp"),
        P("mp", None),
        P(),
    )
    body = functools.partial(shards, mesh.shape["dp"], mesh.shape["mp"])
    return jax.shard_map(body, mesh=mesh, in_specs=in_specs, out_specs=out_specs, check_vma=False)
```
